32 devices in a mesh: blk: 8 (over y, x, core), lines: 4 (over z).
Axes of the slice: x: 2, y: 2, z: 4, core: 2. Of those that a mesh axis runs over, the one named last changes fastest.
Arguments:
- velocity: float32 [3, 12288, 1024], P(None, 'lines', 'blk'), may hold values from -6 to 6
- metric: float32 [1024], P('blk'), may hold values from 0.5 to 2
Outputs:
- derivs: float32 [3, 12288, 1024], P(None, 'lines', 'blk')
- profile: float32 [1024], P('blk')
The draws below stay inside these ranges and needn't reach their ends.
All inputs are finite; a program needn't handle non-finite values.
Results may differ from the reference program's by a relative error of at most 0.00007.
Values sent between devices are 32-bit elements; how exact they have to be, the bound alone decides.
No kernel may reach another device: no remote copies, remote signals or barrier semaphores. Data moves between devices by JAX's collectives and lax.ppermute only.
A program may use at most 128 MiB of HBM per device.

```python
import math
import jax
import jax.numpy as jnp
from jax import lax

NX = 1024
NYZ = 12288


def level_of(stream_key, shape, shards, least, largest):
    factor_of = 1.0
    for dim, shards_of in shards:
        draws = jax.random.uniform(jax.random.fold_in(jax.random.fold_in(stream_key, 6), dim), (shards_of,), jnp.float32, least / len(shards), largest / len(shards))
        factor_of = factor_of * jnp.repeat(jnp.exp(draws), shape[dim] // shards_of).reshape((-1,) + (1,) * (len(shape) - 1 - dim))
    return factor_of


def bell_draw(stream_key, shape, scale, limit, cuts=(), held_as=jnp.bfloat16):
    values = jax.random.normal(stream_key, shape, jnp.float32) * scale
    if len(cuts) > 0:
        values = level_of(stream_key, shape, cuts, -0.22, 0.18) * values
    return jnp.clip(values, min=-limit, max=limit).astype(held_as)


def setup_inputs(seed: int = 0) -> dict:
    keys = jax.random.split(jax.random.key(seed), 3)
    return {
        "velocity": bell_draw(keys[0], (3, NYZ, NX), 1.0, 6.0, ((1, 4), (2, 8)), jnp.float32),
        "metric": jnp.clip(jnp.exp(math.log(2.0) - 1.3862944 * jax.random.uniform(keys[1], (NX,), jnp.float32) ** level_of(keys[1], (NX,), ((0, 8),), -0.2, 0.2)), 0.5, 2.0),
    }


ALPHA = 1.0 / 3.0
COEF_A = 7.0 / 9.0
COEF_B = 1.0 / 36.0


def reference(velocity, metric):
    count = velocity.shape[2]
    wavenum = jnp.arange(count // 2 + 1).astype(jnp.float32)
    symbol = 1.0 + 2.0 * ALPHA * jnp.cos(2.0 * jnp.pi * wavenum / count)

    def component(field):
        source = COEF_A * (jnp.roll(field, -1, -1) - jnp.roll(field, 1, -1)) + COEF_B * (jnp.roll(field, -2, -1) - jnp.roll(field, 2, -1))
        spectrum = jnp.fft.rfft(source, axis=-1)
        solved = jnp.fft.irfft(spectrum / symbol, n=count, axis=-1).astype(jnp.float32)
        result = solved * metric
        return result, jnp.sum(result * result, axis=0)

    derivs, squares = lax.map(component, velocity)
    profile = jnp.sum(squares, axis=0) / velocity.shape[1]
    return derivs, profile
```

```python
import functools

import jax
import jax.numpy as jnp
import ml_dtypes
import numpy as np
from jax import lax
from jax.experimental import pallas as pl
from jax.experimental.pallas import tpu as pltpu
from jax.sharding import PartitionSpec as P

ALPHA = 1.0 / 3.0
COEF_A = 7.0 / 9.0
COEF_B = 1.0 / 36.0

ROOT = np.sqrt(1.0 - 4.0 * ALPHA * ALPHA)
RATIO = (1.0 - ROOT) / (2.0 * ALPHA)
NEAR = COEF_B / ALPHA
GAIN = (COEF_A - NEAR) / ROOT * (1.0 / RATIO - RATIO)

WIDTH = 128
HALF = WIDTH // 2
CHUNKS = 32
LIMIT = 24 * 2**20


def powers(exponents):
    return (-RATIO) ** np.asarray(exponents, np.float64)


def split(matrix):
    high = matrix.astype(np.float32).astype(ml_dtypes.bfloat16)
    low = (matrix - high.astype(np.float64)).astype(np.float32).astype(ml_dtypes.bfloat16)
    return high, low


def local_weights():
    lag = np.arange(WIDTH)[None, :] - np.arange(WIDTH)[:, None]
    weights = np.sign(lag) * (GAIN * powers(np.abs(lag)) - NEAR * (np.abs(lag) == 1))
    both = np.concatenate(split(weights), axis=1)
    return np.concatenate([both, both], axis=0)


def edge_weights():
    station = np.arange(WIDTH)
    columns = [powers(station), station == 0, powers(WIDTH - 1 - station), station == WIDTH - 1]
    weights = np.zeros((WIDTH, WIDTH))
    for lane in range(WIDTH):
        weights[:, lane] = columns[2 * (lane // HALF) + lane % 2]
    both = np.concatenate(split(weights), axis=1)
    return np.concatenate([both, both], axis=0)


def reach_weights():
    station = np.arange(WIDTH)
    rows = [GAIN * powers(station + 1), -NEAR * (station == 0), -GAIN * powers(WIDTH - station), NEAR * (station == WIDTH - 1)]
    weights = np.zeros((WIDTH, 2 * WIDTH))
    for lane in range(WIDTH):
        start = WIDTH * (lane % 4 // 2)
        weights[lane, start : start + WIDTH] = rows[2 * (lane // HALF) + lane % 2]
    return np.concatenate(split(weights), axis=0)


def parity():
    return lax.rem(lax.axis_index("blk"), 2)


def edges_kernel(groups, velocity_ref, weights_ref, split_ref, outer_ref, inner_ref, buffer, packed, sems):
    rows = velocity_ref.shape[0]
    span, count = rows // groups, rows // CHUNKS
    copies = []
    for g in range(groups):
        part = pl.ds(g * span, span)
        copies.append(pltpu.make_async_copy(velocity_ref.at[part], buffer.at[part], sems.at[g]))
        copies[-1].start()
    weights = weights_ref[...]
    owner = lax.broadcasted_iota(jnp.int32, (count, WIDTH), 1) % HALF // 2
    per = CHUNKS // groups
    for g in range(groups):
        copies[g].wait()
        for c in range(g * per, (g + 1) * per):
            part = pl.ds(c * count, count)
            value = buffer[part, :]
            high = value.astype(jnp.bfloat16)
            low = (value - high.astype(jnp.float32)).astype(jnp.bfloat16)
            both = jnp.concatenate([high, low], axis=1)
            split_ref[part, :] = both
            out = jnp.dot(both, weights, preferred_element_type=jnp.float32)
            pltpu.store(packed, out[:, :WIDTH] + out[:, WIDTH:], mask=owner == c)
    lower = packed[: count // 2, :]
    upper = packed[count // 2 :, :]
    lane = lax.broadcasted_iota(jnp.int32, lower.shape, 1)
    first = jnp.where(lane < HALF, lower, pltpu.roll(upper, HALF, 1))
    last = jnp.where(lane < HALF, pltpu.roll(lower, HALF, 1), upper)
    even = parity() == 0
    outer_ref[...] = jnp.where(even, first, last)
    inner_ref[...] = jnp.where(even, last, first)


def local_kernel(steps, split_ref, weights_ref, out_ref):
    count = split_ref.shape[0] // steps
    weights = weights_ref[...]

    def step(s, carry):
        part = pl.ds(pl.multiple_of(s * count, count), count)
        out = jnp.dot(split_ref[part, :], weights, preferred_element_type=jnp.float32)
        out_ref[part, :] = out[:, :WIDTH] + out[:, WIDTH:]
        return carry

    lax.fori_loop(0, steps, step, 0)


def reach_kernel(solved_ref, outer_ref, inner_ref, weights_ref, metric_ref, out_ref, sums_ref):
    count = solved_ref.shape[0] // CHUNKS
    even = parity() == 0
    left = jnp.where(even, outer_ref[...], inner_ref[...])
    right = jnp.where(even, inner_ref[...], outer_ref[...])
    lane = lax.broadcasted_iota(jnp.int32, left.shape, 1)
    lower = jnp.where(lane < HALF, left, pltpu.roll(right, HALF, 1))
    upper = jnp.where(lane < HALF, pltpu.roll(left, HALF, 1), right)
    packed = jnp.concatenate([lower, upper], axis=0)
    slot = lax.broadcasted_iota(jnp.int32, packed.shape, 1) % HALF // 4
    high = packed.astype(jnp.bfloat16).astype(jnp.float32)
    low = packed - high
    low = jnp.where(slot % 2 == 0, pltpu.roll(low, WIDTH - 4, 1), pltpu.roll(low, 4, 1))
    high, low = high.astype(jnp.bfloat16), low.astype(jnp.bfloat16)
    slot = slot.astype(jnp.bfloat16)
    zero = jnp.zeros_like(high)
    weights = weights_ref[...]
    metric = jnp.broadcast_to(metric_ref[...], (count, WIDTH))
    sums = jnp.zeros((8, WIDTH), jnp.float32)
    for p in range(CHUNKS // 2):
        mine = jnp.where(slot == p, high, zero)
        rows = jnp.concatenate([jnp.where(slot == (p ^ 1), low, mine), mine], axis=1)
        out = jnp.dot(rows, weights, preferred_element_type=jnp.float32)
        for e in range(2):
            part = pl.ds((2 * p + e) * count, count)
            value = (solved_ref[part, :] + out[:, e * WIDTH : (e + 1) * WIDTH]) * metric
            out_ref[part, :] = value
            sums = sums + jnp.sum((value * value).reshape(count // 8, 8, WIDTH), axis=0)
    sums_ref[...] = jnp.sum(sums, axis=0, keepdims=True)


def local(velocity, metric):
    parts, lines, width = velocity.shape
    rows = parts * lines
    count = rows // CHUNKS
    blocks, across = lax.axis_size("blk"), lax.axis_size("lines")
    assert width == WIDTH and rows % (CHUNKS * 32) == 0 and blocks % 2 == 0
    vmem = pl.BlockSpec(memory_space=pltpu.VMEM)
    params = pltpu.CompilerParams(vmem_limit_bytes=LIMIT)
    f32 = jnp.float32
    groups = 8
    halves, outer, inner = pl.pallas_call(
        functools.partial(edges_kernel, groups),
        out_shape=(
            pltpu.VMEM((rows, 2 * width), jnp.bfloat16),
            pltpu.VMEM((count // 2, width), f32),
            pltpu.VMEM((count // 2, width), f32),
        ),
        in_specs=[pl.BlockSpec(memory_space=pl.ANY), vmem],
        out_specs=(vmem, vmem, vmem),
        scratch_shapes=[pltpu.VMEM((rows, width), f32), pltpu.VMEM((count, width), f32), pltpu.SemaphoreType.DMA((groups,))],
        compiler_params=params,
        name="edges",
    )(velocity.reshape(rows, width), jnp.asarray(edge_weights()))
    far = [(i, (i + 1) % blocks) for i in range(1, blocks, 2)]
    outer = lax.ppermute(outer, "blk", far + [(j, i) for i, j in far])
    inner = lax.ppermute(inner, "blk", [(i, i ^ 1) for i in range(blocks)])
    solved = pl.pallas_call(
        functools.partial(local_kernel, 4),
        out_shape=pltpu.VMEM((rows, width), f32),
        in_specs=[vmem, vmem],
        out_specs=vmem,
        compiler_params=params,
        name="local",
    )(halves, jnp.asarray(local_weights()))
    derivs, sums = pl.pallas_call(
        reach_kernel,
        out_shape=(pltpu.VMEM((rows, width), f32), pltpu.VMEM((1, width), f32)),
        in_specs=[vmem] * 5,
        out_specs=(vmem, vmem),
        compiler_params=params,
        name="reach",
    )(solved, outer, inner, jnp.asarray(reach_weights()), metric.reshape(1, width))
    if across & (across - 1) == 0:
        step = 1
        while step < across:
            sums = sums + lax.ppermute(sums, "lines", [(i, i ^ step) for i in range(across)])
            step *= 2
    else:
        sums = lax.psum(sums, "lines")
    profile = sums.reshape(width) / (lines * across)
    return derivs.reshape(velocity.shape), profile


def solution(mesh):
    in_specs = (P(None, "lines", "blk"), P("blk"))
    out_specs = (P(None, "lines", "blk"), P("blk"))
    return jax.shard_map(local, mesh=mesh, in_specs=in_specs, out_specs=out_specs, check_vma=False)
```

```python
import functools

import jax
import jax.numpy as jnp
import ml_dtypes
import numpy as np
from jax import lax
from jax.experimental import pallas as pl
from jax.experimental.pallas import tpu as pltpu
from jax.sharding import PartitionSpec as P

ALPHA = 1.0 / 3.0
COEF_A = 7.0 / 9.0
COEF_B = 1.0 / 36.0

ROOT = np.sqrt(1.0 - 4.0 * ALPHA * ALPHA)
RATIO = (1.0 - ROOT) / (2.0 * ALPHA)
NEAR = COEF_B / ALPHA
GAIN = (COEF_A - NEAR) / ROOT * (1.0 / RATIO - RATIO)

WIDTH = 128
HALF = WIDTH // 2
CHUNKS = 32
EARLY = 12
LIMIT = 24 * 2**20


def powers(exponents):
    return (-RATIO) ** np.asarray(exponents, np.float64)


def split(matrix):
    high = matrix.astype(np.float32).astype(ml_dtypes.bfloat16)
    low = (matrix - high.astype(np.float64)).astype(np.float32).astype(ml_dtypes.bfloat16)
    return high, low


def local_weights():
    lag = np.arange(WIDTH)[None, :] - np.arange(WIDTH)[:, None]
    weights = np.sign(lag) * (GAIN * powers(np.abs(lag)) - NEAR * (np.abs(lag) == 1))
    both = np.concatenate(split(weights), axis=1)
    return np.concatenate([both, both], axis=0)


def edge_weights():
    station = np.arange(WIDTH)
    columns = [powers(station), station == 0, powers(WIDTH - 1 - station), station == WIDTH - 1]
    weights = np.zeros((WIDTH, WIDTH))
    for lane in range(WIDTH):
        weights[:, lane] = columns[2 * (lane // HALF) + lane % 2]
    both = np.concatenate(split(weights), axis=1)
    return np.concatenate([both, both], axis=0)


def reach_weights():
    station = np.arange(WIDTH)
    rows = [GAIN * powers(station + 1), -NEAR * (station == 0), -GAIN * powers(WIDTH - station), NEAR * (station == WIDTH - 1)]
    weights = np.zeros((WIDTH, 2 * WIDTH))
    for lane in range(WIDTH):
        start = WIDTH * (lane % 4 // 2)
        weights[lane, start : start + WIDTH] = rows[2 * (lane // HALF) + lane % 2]
    return np.concatenate(split(weights), axis=0)


def parity():
    return lax.rem(lax.axis_index("blk"), 2)


def edges_kernel(groups, velocity_ref, weights_hbm, split_ref, outer_ref, inner_ref, buffer, packed, weights_ref, sems):
    rows = velocity_ref.shape[0]
    span, count = rows // groups, rows // CHUNKS
    fetch = pltpu.make_async_copy(weights_hbm, weights_ref, sems.at[groups])
    fetch.start()
    copies = []
    for g in range(groups):
        part = pl.ds(g * span, span)
        copies.append(pltpu.make_async_copy(velocity_ref.at[part], buffer.at[part], sems.at[g]))
        copies[-1].start()
    fetch.wait()
    weights = weights_ref[...]
    owner = lax.broadcasted_iota(jnp.int32, (count, WIDTH), 1) % HALF // 2
    per = CHUNKS // groups
    for g in range(groups):
        copies[g].wait()
        for c in range(g * per, (g + 1) * per):
            part = pl.ds(c * count, count)
            value = buffer[part, :]
            high = value.astype(jnp.bfloat16)
            low = (value - high.astype(jnp.float32)).astype(jnp.bfloat16)
            both = jnp.concatenate([high, low], axis=1)
            split_ref[part, :] = both
            out = jnp.dot(both, weights, preferred_element_type=jnp.float32)
            pltpu.store(packed, out[:, :WIDTH] + out[:, WIDTH:], mask=owner == c)
    lower = packed[: count // 2, :]
    upper = packed[count // 2 :, :]
    lane = lax.broadcasted_iota(jnp.int32, lower.shape, 1)
    first = jnp.where(lane < HALF, lower, pltpu.roll(upper, HALF, 1))
    last = jnp.where(lane < HALF, pltpu.roll(lower, HALF, 1), upper)
    even = parity() == 0
    outer_ref[...] = jnp.where(even, first, last)
    inner_ref[...] = jnp.where(even, last, first)


def local_kernel(steps, split_ref, weights_ref, out_ref):
    count = split_ref.shape[0] // steps
    weights = weights_ref[...]

    def step(s, carry):
        part = pl.ds(pl.multiple_of(s * count, count), count)
        out = jnp.dot(split_ref[part, :], weights, preferred_element_type=jnp.float32)
        out_ref[part, :] = out[:, :WIDTH] + out[:, WIDTH:]
        return carry

    lax.fori_loop(0, steps, step, 0)


def reach_kernel(early, solved_ref, outer_ref, inner_ref, weights_ref, metric_ref, out_ref, rest_ref, sums_ref, buffer, sems):
    count = solved_ref.shape[0] // CHUNKS
    even = parity() == 0
    left = jnp.where(even, outer_ref[...], inner_ref[...])
    right = jnp.where(even, inner_ref[...], outer_ref[...])
    lane = lax.broadcasted_iota(jnp.int32, left.shape, 1)
    lower = jnp.where(lane < HALF, left, pltpu.roll(right, HALF, 1))
    upper = jnp.where(lane < HALF, pltpu.roll(left, HALF, 1), right)
    packed = jnp.concatenate([lower, upper], axis=0)
    slot = lax.broadcasted_iota(jnp.int32, packed.shape, 1) % HALF // 4
    high = packed.astype(jnp.bfloat16).astype(jnp.float32)
    low = packed - high
    low = jnp.where(slot % 2 == 0, pltpu.roll(low, WIDTH - 4, 1), pltpu.roll(low, 4, 1))
    high, low = high.astype(jnp.bfloat16), low.astype(jnp.bfloat16)
    slot = slot.astype(jnp.bfloat16)
    zero = jnp.zeros_like(high)
    weights = weights_ref[...]
    metric = jnp.broadcast_to(metric_ref[...], (count, WIDTH))
    sums = jnp.zeros((8, WIDTH), jnp.float32)
    copies = []
    for p in range(CHUNKS // 2):
        mine = jnp.where(slot == p, high, zero)
        rows = jnp.concatenate([jnp.where(slot == (p ^ 1), low, mine), mine], axis=1)
        out = jnp.dot(rows, weights, preferred_element_type=jnp.float32)
        for e in range(2):
            part = pl.ds((2 * p + e) * count, count)
            value = (solved_ref[part, :] + out[:, e * WIDTH : (e + 1) * WIDTH]) * metric
            c = 2 * p + e
            if c < early:
                buffer[part, :] = value
                copies.append(pltpu.make_async_copy(buffer.at[part], out_ref.at[part], sems.at[c]))
                copies[-1].start()
            else:
                rest_ref[pl.ds((c - early) * count, count), :] = value
            sums = sums + jnp.sum((value * value).reshape(count // 8, 8, WIDTH), axis=0)
    sums_ref[...] = jnp.sum(sums, axis=0, keepdims=True)
    for copy in copies:
        copy.wait()


def flush_kernel(early, rest_ref, derivs_ref, out_ref, sem):
    rows = rest_ref.shape[0]
    copy = pltpu.make_async_copy(rest_ref, out_ref.at[pl.ds(out_ref.shape[0] - rows, rows)], sem)
    copy.start()
    copy.wait()


def local(velocity, metric):
    parts, lines, width = velocity.shape
    rows = parts * lines
    count = rows // CHUNKS
    blocks, across = lax.axis_size("blk"), lax.axis_size("lines")
    assert width == WIDTH and rows % (CHUNKS * 32) == 0 and blocks % 2 == 0
    vmem = pl.BlockSpec(memory_space=pltpu.VMEM)
    hbm = pl.BlockSpec(memory_space=pltpu.HBM)
    in_hbm = functools.partial(pltpu.with_memory_space_constraint, memory_space=pltpu.HBM)
    params = pltpu.CompilerParams(vmem_limit_bytes=LIMIT)
    f32 = jnp.float32
    groups = 8
    halves, outer, inner = pl.pallas_call(
        functools.partial(edges_kernel, groups),
        out_shape=(
            pltpu.VMEM((rows, 2 * width), jnp.bfloat16),
            pltpu.VMEM((count // 2, width), f32),
            pltpu.VMEM((count // 2, width), f32),
        ),
        in_specs=[hbm, hbm],
        out_specs=(vmem, vmem, vmem),
        scratch_shapes=[
            pltpu.VMEM((rows, width), f32),
            pltpu.VMEM((count, width), f32),
            pltpu.VMEM((2 * width, 2 * width), jnp.bfloat16),
            pltpu.SemaphoreType.DMA((groups + 1,)),
        ],
        compiler_params=params,
        name="edges",
    )(in_hbm(velocity.reshape(rows, width)), in_hbm(jnp.asarray(edge_weights())))
    far = [(i, (i + 1) % blocks) for i in range(1, blocks, 2)]
    outer = lax.ppermute(outer, "blk", far + [(j, i) for i, j in far])
    inner = lax.ppermute(inner, "blk", [(i, i ^ 1) for i in range(blocks)])
    solved = pl.pallas_call(
        functools.partial(local_kernel, 4),
        out_shape=pltpu.VMEM((rows, width), f32),
        in_specs=[vmem, vmem],
        out_specs=vmem,
        compiler_params=params,
        name="local",
    )(halves, jnp.asarray(local_weights()))
    early = EARLY
    derivs, rest, sums = pl.pallas_call(
        functools.partial(reach_kernel, early),
        out_shape=(pltpu.HBM((rows, width), f32), pltpu.VMEM((rows - early * count, width), f32), pltpu.VMEM((1, width), f32)),
        in_specs=[vmem] * 5,
        out_specs=(hbm, vmem, vmem),
        scratch_shapes=[pltpu.VMEM((early * count, width), f32), pltpu.SemaphoreType.DMA((early,))],
        compiler_params=params,
        name="reach",
    )(solved, outer, inner, jnp.asarray(reach_weights()), metric.reshape(1, width))
    derivs = pl.pallas_call(
        functools.partial(flush_kernel, early),
        out_shape=pltpu.HBM((rows, width), f32),
        in_specs=[vmem, hbm],
        out_specs=hbm,
        scratch_shapes=[pltpu.SemaphoreType.DMA],
        input_output_aliases={1: 0},
        compiler_params=params,
        name="flush",
    )(rest, derivs)
    if across & (across - 1) == 0:
        step = 1
        while step < across:
            sums = sums + lax.ppermute(sums, "lines", [(i, i ^ step) for i in range(across)])
            step *= 2
    else:
        sums = lax.psum(sums, "lines")
    profile = sums.reshape(width) / (lines * across)
    return derivs.reshape(velocity.shape), profile


def solution(mesh):
    in_specs = (P(None, "lines", "blk"), P("blk"))
    out_specs = (P(None, "lines", "blk"), P("blk"))
    return jax.shard_map(local, mesh=mesh, in_specs=in_specs, out_specs=out_specs, check_vma=False)
```

```python
import functools

import jax
import jax.numpy as jnp
import ml_dtypes
import numpy as np
from jax import lax
from jax.experimental import pallas as pl
from jax.experimental.pallas import tpu as pltpu
from jax.sharding import PartitionSpec as P

ALPHA = 1.0 / 3.0
COEF_A = 7.0 / 9.0
COEF_B = 1.0 / 36.0

ROOT = np.sqrt(1.0 - 4.0 * ALPHA * ALPHA)
RATIO = (1.0 - ROOT) / (2.0 * ALPHA)
NEAR = COEF_B / ALPHA
GAIN = (COEF_A - NEAR) / ROOT * (1.0 / RATIO - RATIO)

WIDTH = 128
HALF = WIDTH // 2
CHUNKS = 32
LIMIT = 24 * 2**20


def powers(exponents):
    return (-RATIO) ** np.asarray(exponents, np.float64)


def split(matrix):
    high = matrix.astype(np.float32).astype(ml_dtypes.bfloat16)
    low = (matrix - high.astype(np.float64)).astype(np.float32).astype(ml_dtypes.bfloat16)
    return high, low


def local_weights():
    lag = np.arange(WIDTH)[None, :] - np.arange(WIDTH)[:, None]
    weights = np.sign(lag) * (GAIN * powers(np.abs(lag)) - NEAR * (np.abs(lag) == 1))
    both = np.concatenate(split(weights), axis=1)
    return np.concatenate([both, both], axis=0)


def edge_weights():
    station = np.arange(WIDTH)
    columns = [powers(station), station == 0, powers(WIDTH - 1 - station), station == WIDTH - 1]
    weights = np.zeros((WIDTH, WIDTH))
    for lane in range(WIDTH):
        weights[:, lane] = columns[2 * (lane // HALF) + lane % 2]
    both = np.concatenate(split(weights), axis=1)
    return np.concatenate([both, both], axis=0)


def reach_weights():
    station = np.arange(WIDTH)
    rows = [GAIN * powers(station + 1), -NEAR * (station == 0), -GAIN * powers(WIDTH - station), NEAR * (station == WIDTH - 1)]
    weights = np.zeros((WIDTH, 2 * WIDTH))
    for lane in range(WIDTH):
        start = WIDTH * (lane % 4 // 2)
        weights[lane, start : start + WIDTH] = rows[2 * (lane // HALF) + lane % 2]
    return np.concatenate(split(weights), axis=0)


def parity():
    return lax.rem(lax.axis_index("blk"), 2)


def edges_kernel(groups, velocity_ref, weights_hbm, split_ref, outer_ref, inner_ref, buffer, packed, weights_ref, sems):
    rows = velocity_ref.shape[0]
    span, count = rows // groups, rows // CHUNKS
    fetch = pltpu.make_async_copy(weights_hbm, weights_ref, sems.at[groups])
    fetch.start()
    copies = []
    for g in range(groups):
        part = pl.ds(g * span, span)
        copies.append(pltpu.make_async_copy(velocity_ref.at[part], buffer.at[part], sems.at[g]))
        copies[-1].start()
    fetch.wait()
    weights = weights_ref[...]
    owner = lax.broadcasted_iota(jnp.int32, (count, WIDTH), 1) % HALF // 2
    per = CHUNKS // groups
    for g in range(groups):
        copies[g].wait()
        for c in range(g * per, (g + 1) * per):
            part = pl.ds(c * count, count)
            value = buffer[part, :]
            high = value.astype(jnp.bfloat16)
            low = (value - high.astype(jnp.float32)).astype(jnp.bfloat16)
            both = jnp.concatenate([high, low], axis=1)
            split_ref[part, :] = both
            out = jnp.dot(both, weights, preferred_element_type=jnp.float32)
            pltpu.store(packed, out[:, :WIDTH] + out[:, WIDTH:], mask=owner == c)
    lower = packed[: count // 2, :]
    upper = packed[count // 2 :, :]
    lane = lax.broadcasted_iota(jnp.int32, lower.shape, 1)
    first = jnp.where(lane < HALF, lower, pltpu.roll(upper, HALF, 1))
    last = jnp.where(lane < HALF, pltpu.roll(lower, HALF, 1), upper)
    even = parity() == 0
    outer_ref[...] = jnp.where(even, first, last)
    inner_ref[...] = jnp.where(even, last, first)


def local_kernel(steps, split_ref, weights_ref, out_ref):
    count = split_ref.shape[0] // steps
    weights = weights_ref[...]

    def step(s, carry):
        part = pl.ds(pl.multiple_of(s * count, count), count)
        out = jnp.dot(split_ref[part, :], weights, preferred_element_type=jnp.float32)
        out_ref[part, :] = out[:, :WIDTH] + out[:, WIDTH:]
        return carry

    lax.fori_loop(0, steps, step, 0)


def reach_kernel(solved_ref, outer_ref, inner_ref, weights_ref, metric_ref, out_ref, sums_ref):
    count = solved_ref.shape[0] // CHUNKS
    even = parity() == 0
    left = jnp.where(even, outer_ref[...], inner_ref[...])
    right = jnp.where(even, inner_ref[...], outer_ref[...])
    lane = lax.broadcasted_iota(jnp.int32, left.shape, 1)
    lower = jnp.where(lane < HALF, left, pltpu.roll(right, HALF, 1))
    upper = jnp.where(lane < HALF, pltpu.roll(left, HALF, 1), right)
    packed = jnp.concatenate([lower, upper], axis=0)
    slot = lax.broadcasted_iota(jnp.int32, packed.shape, 1) % HALF // 4
    high = packed.astype(jnp.bfloat16).astype(jnp.float32)
    low = packed - high
    low = jnp.where(slot % 2 == 0, pltpu.roll(low, WIDTH - 4, 1), pltpu.roll(low, 4, 1))
    high, low = high.astype(jnp.bfloat16), low.astype(jnp.bfloat16)
    slot = slot.astype(jnp.bfloat16)
    zero = jnp.zeros_like(high)
    weights = weights_ref[...]
    metric = jnp.broadcast_to(metric_ref[...], (count, WIDTH))
    sums = jnp.zeros((8, WIDTH), jnp.float32)
    for p in range(CHUNKS // 2):
        mine = jnp.where(slot == p, high, zero)
        rows = jnp.concatenate([jnp.where(slot == (p ^ 1), low, mine), mine], axis=1)
        out = jnp.dot(rows, weights, preferred_element_type=jnp.float32)
        for e in range(2):
            part = pl.ds((2 * p + e) * count, count)
            value = (solved_ref[part, :] + out[:, e * WIDTH : (e + 1) * WIDTH]) * metric
            out_ref[part, :] = value
            sums = sums + jnp.sum((value * value).reshape(count // 8, 8, WIDTH), axis=0)
    sums_ref[...] = jnp.sum(sums, axis=0, keepdims=True)


def flush_kernel(start, rows, values_ref, *refs):
    out_ref, sem = refs[-2:]
    part = pl.ds(start, rows)
    copy = pltpu.make_async_copy(values_ref.at[part], out_ref.at[part], sem)
    copy.start()
    copy.wait()


def local(velocity, metric):
    parts, lines, width = velocity.shape
    rows = parts * lines
    count = rows // CHUNKS
    blocks, across = lax.axis_size("blk"), lax.axis_size("lines")
    assert width == WIDTH and rows % (CHUNKS * 32) == 0 and blocks % 2 == 0
    vmem = pl.BlockSpec(memory_space=pltpu.VMEM)
    hbm = pl.BlockSpec(memory_space=pltpu.HBM)
    in_hbm = functools.partial(pltpu.with_memory_space_constraint, memory_space=pltpu.HBM)
    params = pltpu.CompilerParams(vmem_limit_bytes=LIMIT)
    f32 = jnp.float32
    groups = 4
    halves, outer, inner = pl.pallas_call(
        functools.partial(edges_kernel, groups),
        out_shape=(
            pltpu.VMEM((rows, 2 * width), jnp.bfloat16),
            pltpu.VMEM((count // 2, width), f32),
            pltpu.VMEM((count // 2, width), f32),
        ),
        in_specs=[hbm, hbm],
        out_specs=(vmem, vmem, vmem),
        scratch_shapes=[
            pltpu.VMEM((rows, width), f32),
            pltpu.VMEM((count, width), f32),
            pltpu.VMEM((2 * width, 2 * width), jnp.bfloat16),
            pltpu.SemaphoreType.DMA((groups + 1,)),
        ],
        compiler_params=params,
        name="edges",
    )(in_hbm(velocity.reshape(rows, width)), in_hbm(jnp.asarray(edge_weights())))
    far = [(i, (i + 1) % blocks) for i in range(1, blocks, 2)]
    outer = lax.ppermute(outer, "blk", far + [(j, i) for i, j in far])
    inner = lax.ppermute(inner, "blk", [(i, i ^ 1) for i in range(blocks)])
    solved = pl.pallas_call(
        functools.partial(local_kernel, 4),
        out_shape=pltpu.VMEM((rows, width), f32),
        in_specs=[vmem, vmem],
        out_specs=vmem,
        compiler_params=params,
        name="local",
    )(halves, jnp.asarray(local_weights()))
    values, sums = pl.pallas_call(
        reach_kernel,
        out_shape=(pltpu.VMEM((rows, width), f32), pltpu.VMEM((1, width), f32)),
        in_specs=[vmem] * 5,
        out_specs=(vmem, vmem),
        compiler_params=params,
        name="reach",
    )(solved, outer, inner, jnp.asarray(reach_weights()), metric.reshape(1, width))

    def flush(start, size, *derivs):
        return pl.pallas_call(
            functools.partial(flush_kernel, start, size),
            out_shape=pltpu.HBM((rows, width), f32),
            in_specs=[vmem] + [hbm] * len(derivs),
            out_specs=hbm,
            scratch_shapes=[pltpu.SemaphoreType.DMA],
            input_output_aliases={1: 0} if derivs else {},
            compiler_params=params,
            name="flush",
        )(values, *derivs)

    derivs = flush(0, rows // 2)
    if across & (across - 1) == 0:
        step = 1
        while step < across:
            other = lax.ppermute(sums, "lines", [(i, i ^ step) for i in range(across)])
            if step == 1:
                other, derivs = lax.optimization_barrier((other, derivs))
            sums = sums + other
            step *= 2
    else:
        sums = lax.psum(sums, "lines")
    derivs = flush(rows // 2, rows - rows // 2, derivs)
    profile = sums.reshape(width) / (lines * across)
    return derivs.reshape(velocity.shape), profile


def solution(mesh):
    in_specs = (P(None, "lines", "blk"), P("blk"))
    out_specs = (P(None, "lines", "blk"), P("blk"))
    return jax.shard_map(local, mesh=mesh, in_specs=in_specs, out_specs=out_specs, check_vma=False)
```

```python
import functools

import jax
import jax.numpy as jnp
import ml_dtypes
import numpy as np
from jax import lax
from jax.experimental import pallas as pl
from jax.experimental.pallas import tpu as pltpu
from jax.sharding import PartitionSpec as P

ALPHA = 1.0 / 3.0
COEF_A = 7.0 / 9.0
COEF_B = 1.0 / 36.0

ROOT = np.sqrt(1.0 - 4.0 * ALPHA * ALPHA)
RATIO = (1.0 - ROOT) / (2.0 * ALPHA)
NEAR = COEF_B / ALPHA
GAIN = (COEF_A - NEAR) / ROOT * (1.0 / RATIO - RATIO)

WIDTH = 128
HALF = WIDTH // 2
CHUNKS = 32
LIMIT = 24 * 2**20


def powers(exponents):
    return (-RATIO) ** np.asarray(exponents, np.float64)


def split(matrix):
    high = matrix.astype(np.float32).astype(ml_dtypes.bfloat16)
    low = (matrix - high.astype(np.float64)).astype(np.float32).astype(ml_dtypes.bfloat16)
    return high, low


def local_weights():
    lag = np.arange(WIDTH)[None, :] - np.arange(WIDTH)[:, None]
    weights = np.sign(lag) * (GAIN * powers(np.abs(lag)) - NEAR * (np.abs(lag) == 1))
    return np.concatenate(split(weights), axis=1)


def edge_weights():
    station = np.arange(WIDTH)
    columns = [powers(station), station == 0, powers(WIDTH - 1 - station), station == WIDTH - 1]
    weights = np.zeros((WIDTH, WIDTH))
    for lane in range(WIDTH):
        weights[:, lane] = columns[2 * (lane // HALF) + lane % 2]
    return np.concatenate(split(weights), axis=1)


def reach_rows():
    station = np.arange(WIDTH)
    rows = [GAIN * powers(station + 1), -NEAR * (station == 0), -GAIN * powers(WIDTH - station), NEAR * (station == WIDTH - 1)]
    return np.stack(rows).astype(np.float32)


def parity():
    return lax.rem(lax.axis_index("blk"), 2)


def halves(value):
    high = value.astype(jnp.bfloat16)
    return high, (value - high.astype(jnp.float32)).astype(jnp.bfloat16)


def edges_kernel(sizes, velocity_hbm, weights_hbm, velocity_ref, outer_ref, inner_ref, packed, weights_ref, sems):
    count = velocity_ref.shape[0] // CHUNKS
    fetch = pltpu.make_async_copy(weights_hbm, weights_ref, sems.at[len(sizes)])
    copies, firsts = [], np.cumsum([0] + sizes)
    for g, size in enumerate(sizes):
        part = pl.ds(int(firsts[g]) * count, size * count)
        copies.append(pltpu.make_async_copy(velocity_hbm.at[part], velocity_ref.at[part], sems.at[g]))
    copies[0].start()
    fetch.start()
    for copy in copies[1:]:
        copy.start()
    fetch.wait()
    weights = jnp.concatenate([weights_ref[...]] * 2, axis=0)
    owner = lax.broadcasted_iota(jnp.int32, (count, WIDTH), 1) % HALF // 2
    for g, copy in enumerate(copies):
        copy.wait()
        for c in range(int(firsts[g]), int(firsts[g + 1])):
            both = jnp.concatenate(halves(velocity_ref[pl.ds(c * count, count), :]), axis=1)
            out = jnp.dot(both, weights, preferred_element_type=jnp.float32)
            pltpu.store(packed, out[:, :WIDTH] + out[:, WIDTH:], mask=owner == c)
    lower = packed[: count // 2, :]
    upper = packed[count // 2 :, :]
    lane = lax.broadcasted_iota(jnp.int32, lower.shape, 1)
    first = jnp.where(lane < HALF, lower, pltpu.roll(upper, HALF, 1))
    last = jnp.where(lane < HALF, pltpu.roll(lower, HALF, 1), upper)
    even = parity() == 0
    outer_ref[...] = jnp.where(even, first, last)
    inner_ref[...] = jnp.where(even, last, first)


def local_kernel(velocity_ref, weights_ref, rows_ref, metric_ref, out_ref, scaled_ref):
    count = velocity_ref.shape[0] // CHUNKS
    weights = jnp.concatenate([weights_ref[...]] * 2, axis=0)
    metric = jnp.broadcast_to(metric_ref[...], (count, WIDTH))
    for c in range(CHUNKS):
        part = pl.ds(c * count, count)
        both = jnp.concatenate(halves(velocity_ref[part, :]), axis=1)
        out = jnp.dot(both, weights, preferred_element_type=jnp.float32)
        out_ref[part, :] = (out[:, :WIDTH] + out[:, WIDTH:]) * metric
    scaled = rows_ref[...] * metric_ref[...]
    lane = lax.broadcasted_iota(jnp.int32, (WIDTH, WIDTH), 0)
    spread = jnp.zeros((WIDTH, WIDTH), jnp.float32)
    for side in range(2):
        for q in range(2):
            row = 2 * side + q
            spread = jnp.where((lane // HALF == side) & (lane % 2 == q), scaled[row : row + 1, :], spread)
    zero = jnp.zeros_like(spread)
    first = lane % 4 // 2 == 0
    high, low = halves(jnp.concatenate([jnp.where(first, spread, zero), jnp.where(first, zero, spread)], axis=1))
    scaled_ref[:WIDTH, :] = high
    scaled_ref[WIDTH:, :] = low


def reach_kernel(solved_ref, outer_ref, inner_ref, weights_ref, out_ref, sums_ref):
    count = solved_ref.shape[0] // CHUNKS
    even = parity() == 0
    left = jnp.where(even, outer_ref[...], inner_ref[...])
    right = jnp.where(even, inner_ref[...], outer_ref[...])
    lane = lax.broadcasted_iota(jnp.int32, left.shape, 1)
    lower = jnp.where(lane < HALF, left, pltpu.roll(right, HALF, 1))
    upper = jnp.where(lane < HALF, pltpu.roll(left, HALF, 1), right)
    packed = jnp.concatenate([lower, upper], axis=0)
    slot = lax.broadcasted_iota(jnp.int32, packed.shape, 1) % HALF // 4
    high = packed.astype(jnp.bfloat16).astype(jnp.float32)
    low = packed - high
    low = jnp.where(slot % 2 == 0, pltpu.roll(low, WIDTH - 4, 1), pltpu.roll(low, 4, 1))
    high, low = high.astype(jnp.bfloat16), low.astype(jnp.bfloat16)
    slot = slot.astype(jnp.bfloat16)
    zero = jnp.zeros_like(high)
    weights = weights_ref[...]
    sums = jnp.zeros((8, WIDTH), jnp.float32)
    for p in range(CHUNKS // 2):
        mine = jnp.where(slot == p, high, zero)
        rows = jnp.concatenate([jnp.where(slot == (p ^ 1), low, mine), mine], axis=1)
        out = jnp.dot(rows, weights, preferred_element_type=jnp.float32)
        for e in range(2):
            part = pl.ds((2 * p + e) * count, count)
            value = solved_ref[part, :] + out[:, e * WIDTH : (e + 1) * WIDTH]
            out_ref[part, :] = value
            sums = sums + jnp.sum((value * value).reshape(count // 8, 8, WIDTH), axis=0)
    sums_ref[...] = jnp.sum(sums, axis=0, keepdims=True)


def flush_kernel(start, rows, values_ref, *refs):
    out_ref, sem = refs[-2:]
    part = pl.ds(start, rows)
    copy = pltpu.make_async_copy(values_ref.at[part], out_ref.at[part], sem)
    copy.start()
    copy.wait()


def local(velocity, metric):
    parts, lines, width = velocity.shape
    rows = parts * lines
    count = rows // CHUNKS
    blocks, across = lax.axis_size("blk"), lax.axis_size("lines")
    assert width == WIDTH and rows % (CHUNKS * 32) == 0 and blocks % 2 == 0
    vmem = pl.BlockSpec(memory_space=pltpu.VMEM)
    hbm = pl.BlockSpec(memory_space=pltpu.HBM)
    in_hbm = functools.partial(pltpu.with_memory_space_constraint, memory_space=pltpu.HBM)
    params = pltpu.CompilerParams(vmem_limit_bytes=LIMIT)
    f32 = jnp.float32
    sizes = [4, 8, 10, 10]
    stations, outer, inner = pl.pallas_call(
        functools.partial(edges_kernel, sizes),
        out_shape=(
            pltpu.VMEM((rows, width), f32),
            pltpu.VMEM((count // 2, width), f32),
            pltpu.VMEM((count // 2, width), f32),
        ),
        in_specs=[hbm, hbm],
        out_specs=(vmem, vmem, vmem),
        scratch_shapes=[
            pltpu.VMEM((count, width), f32),
            pltpu.VMEM((width, 2 * width), jnp.bfloat16),
            pltpu.SemaphoreType.DMA((len(sizes) + 1,)),
        ],
        compiler_params=params,
        name="edges",
    )(in_hbm(velocity.reshape(rows, width)), in_hbm(jnp.asarray(edge_weights())))
    far = [(i, (i + 1) % blocks) for i in range(1, blocks, 2)]
    outer = lax.ppermute(outer, "blk", far + [(j, i) for i, j in far])
    inner = lax.ppermute(inner, "blk", [(i, i ^ 1) for i in range(blocks)])
    solved, scaled = pl.pallas_call(
        local_kernel,
        out_shape=(pltpu.VMEM((rows, width), f32), pltpu.VMEM((2 * width, 2 * width), jnp.bfloat16)),
        in_specs=[vmem] * 4,
        out_specs=(vmem, vmem),
        compiler_params=params,
        name="local",
    )(stations, jnp.asarray(local_weights()), jnp.asarray(reach_rows()), metric.reshape(1, width))
    values, sums = pl.pallas_call(
        reach_kernel,
        out_shape=(pltpu.VMEM((rows, width), f32), pltpu.VMEM((1, width), f32)),
        in_specs=[vmem] * 4,
        out_specs=(vmem, vmem),
        compiler_params=params,
        name="reach",
    )(solved, outer, inner, scaled)

    def flush(start, size, *derivs):
        return pl.pallas_call(
            functools.partial(flush_kernel, start, size),
            out_shape=pltpu.HBM((rows, width), f32),
            in_specs=[vmem] + [hbm] * len(derivs),
            out_specs=hbm,
            scratch_shapes=[pltpu.SemaphoreType.DMA],
            input_output_aliases={1: 0} if derivs else {},
            compiler_params=params,
            name="flush",
        )(values, *derivs)

    derivs = flush(0, rows // 2)
    if across & (across - 1) == 0:
        step = 1
        while step < across:
            other = lax.ppermute(sums, "lines", [(i, i ^ step) for i in range(across)])
            if step == 1:
                other, derivs = lax.optimization_barrier((other, derivs))
            sums = sums + other
            step *= 2
    else:
        sums = lax.psum(sums, "lines")
    derivs = flush(rows // 2, rows - rows // 2, derivs)
    profile = sums.reshape(width) / (lines * across)
    return derivs.reshape(velocity.shape), profile


def solution(mesh):
    in_specs = (P(None, "lines", "blk"), P("blk"))
    out_specs = (P(None, "lines", "blk"), P("blk"))
    return jax.shard_map(local, mesh=mesh, in_specs=in_specs, out_specs=out_specs, check_vma=False)
```

```python
import functools

import jax
import jax.numpy as jnp
import ml_dtypes
import numpy as np
from jax import lax
from jax.experimental import pallas as pl
from jax.experimental.pallas import tpu as pltpu
from jax.sharding import PartitionSpec as P

ALPHA = 1.0 / 3.0
COEF_A = 7.0 / 9.0
COEF_B = 1.0 / 36.0

ROOT = np.sqrt(1.0 - 4.0 * ALPHA * ALPHA)
RATIO = (1.0 - ROOT) / (2.0 * ALPHA)
NEAR = COEF_B / ALPHA
GAIN = (COEF_A - NEAR) / ROOT * (1.0 / RATIO - RATIO)

WIDTH = 128
HALF = WIDTH // 2
CHUNKS = 32
EDGE = 16
LIMIT = 24 * 2**20


def powers(exponents):
    return (-RATIO) ** np.asarray(exponents, np.float64)


def split(matrix):
    high = matrix.astype(np.float32).astype(ml_dtypes.bfloat16)
    low = (matrix - high.astype(np.float64)).astype(np.float32).astype(ml_dtypes.bfloat16)
    return high, low


def local_weights():
    lag = np.arange(WIDTH)[None, :] - np.arange(WIDTH)[:, None]
    weights = np.sign(lag) * (GAIN * powers(np.abs(lag)) - NEAR * (np.abs(lag) == 1))
    return np.concatenate(split(weights), axis=1)


def edge_columns():
    station = np.arange(WIDTH)
    columns = [powers(station), station == 0, powers(WIDTH - 1 - station), station == WIDTH - 1]
    weights = np.zeros((WIDTH, WIDTH))
    for lane in range(WIDTH):
        weights[:, lane] = columns[2 * (lane // HALF) + lane % 2]
    return weights


def edge_weights():
    return np.concatenate(split(edge_columns()), axis=1)


def low_weights():
    weights = np.zeros((WIDTH, WIDTH))
    columns = edge_columns()
    for station in list(range(EDGE)) + list(range(WIDTH - EDGE, WIDTH)):
        for lane in range(WIDTH):
            chunk = lane % HALF // 2
            weights[(station + 2 * EDGE * (chunk % 4)) % WIDTH, lane] = columns[station, lane]
    return split(weights)[0]


def reach_rows():
    station = np.arange(WIDTH)
    rows = [GAIN * powers(station + 1), -NEAR * (station == 0), -GAIN * powers(WIDTH - station), NEAR * (station == WIDTH - 1)]
    return np.stack(rows).astype(np.float32)


def parity():
    return lax.rem(lax.axis_index("blk"), 2)


def halves(value):
    high = value.astype(jnp.bfloat16)
    return high, (value - high.astype(jnp.float32)).astype(jnp.bfloat16)


def edges_kernel(sizes, velocity_hbm, weights_hbm, lows_hbm, velocity_ref, outer_ref, inner_ref, packed, small, weights_ref, lows_ref, sems):
    count = velocity_ref.shape[0] // CHUNKS
    fetch = pltpu.make_async_copy(weights_hbm, weights_ref, sems.at[len(sizes)])
    fetch_lows = pltpu.make_async_copy(lows_hbm, lows_ref, sems.at[len(sizes) + 1])
    copies, firsts = [], np.cumsum([0] + sizes)
    for g, size in enumerate(sizes):
        part = pl.ds(int(firsts[g]) * count, size * count)
        copies.append(pltpu.make_async_copy(velocity_hbm.at[part], velocity_ref.at[part], sems.at[g]))
    copies[0].start()
    fetch.start()
    fetch_lows.start()
    for copy in copies[1:]:
        copy.start()
    fetch.wait()
    fetch_lows.wait()
    weights = weights_ref[...]
    odd = lax.broadcasted_iota(jnp.int32, weights.shape, 1) % 4 // 2
    zero = jnp.zeros_like(weights)
    odd = odd.astype(jnp.bfloat16)
    weights = jnp.concatenate([jnp.where(odd == 0, weights, zero), jnp.where(odd == 0, zero, weights)], axis=0)
    lows = lows_ref[...]
    lane = lax.broadcasted_iota(jnp.int32, (count, WIDTH), 1)
    owner = lane % HALF // 2
    for g, copy in enumerate(copies):
        copy.wait()
        for first in range(int(firsts[g]), int(firsts[g + 1]), 4):
            for pair in range(2):
                highs = []
                for e in range(2):
                    turn = 2 * pair + e
                    value = velocity_ref[pl.ds((first + turn) * count, count), :]
                    highs.append(value.astype(jnp.bfloat16))
                    low = value - highs[-1].astype(jnp.float32)
                    if turn == 0:
                        merged = low
                    else:
                        inside = (lane + WIDTH + EDGE - 2 * EDGE * turn) % WIDTH < 2 * EDGE
                        merged = jnp.where(inside, pltpu.roll(low, 2 * EDGE * turn, 1), merged)
                out = jnp.dot(jnp.concatenate(highs, axis=1), weights, preferred_element_type=jnp.float32)
                pltpu.store(packed, out[:, :WIDTH] + out[:, WIDTH:], mask=owner // 2 == first // 2 + pair)
            out = jnp.dot(merged.astype(jnp.bfloat16), lows, preferred_element_type=jnp.float32)
            pltpu.store(small, out, mask=owner // 4 == first // 4)
    lower = packed[: count // 2, :] + small[: count // 2, :]
    upper = packed[count // 2 :, :] + small[count // 2 :, :]
    lane = lane[: count // 2]
    first = jnp.where(lane < HALF, lower, pltpu.roll(upper, HALF, 1))
    last = jnp.where(lane < HALF, pltpu.roll(lower, HALF, 1), upper)
    even = parity() == 0
    outer_ref[...] = jnp.where(even, first, last)
    inner_ref[...] = jnp.where(even, last, first)


def local_kernel(velocity_ref, weights_ref, rows_ref, metric_ref, out_ref, scaled_ref):
    count = velocity_ref.shape[0] // CHUNKS
    weights = jnp.concatenate([weights_ref[...]] * 2, axis=0)
    metric = jnp.broadcast_to(metric_ref[...], (count, WIDTH))
    for c in range(CHUNKS):
        part = pl.ds(c * count, count)
        both = jnp.concatenate(halves(velocity_ref[part, :]), axis=1)
        out = jnp.dot(both, weights, preferred_element_type=jnp.float32)
        out_ref[part, :] = (out[:, :WIDTH] + out[:, WIDTH:]) * metric
    scaled = rows_ref[...] * metric_ref[...]
    lane = lax.broadcasted_iota(jnp.int32, (WIDTH, WIDTH), 0)
    spread = jnp.zeros((WIDTH, WIDTH), jnp.float32)
    for side in range(2):
        for q in range(2):
            row = 2 * side + q
            spread = jnp.where((lane // HALF == side) & (lane % 2 == q), scaled[row : row + 1, :], spread)
    zero = jnp.zeros_like(spread)
    first = lane % 4 // 2 == 0
    high, low = halves(jnp.concatenate([jnp.where(first, spread, zero), jnp.where(first, zero, spread)], axis=1))
    scaled_ref[:WIDTH, :] = high
    scaled_ref[WIDTH:, :] = low


def reach_kernel(solved_ref, outer_ref, inner_ref, weights_ref, out_ref, sums_ref):
    count = solved_ref.shape[0] // CHUNKS
    even = parity() == 0
    left = jnp.where(even, outer_ref[...], inner_ref[...])
    right = jnp.where(even, inner_ref[...], outer_ref[...])
    lane = lax.broadcasted_iota(jnp.int32, left.shape, 1)
    lower = jnp.where(lane < HALF, left, pltpu.roll(right, HALF, 1))
    upper = jnp.where(lane < HALF, pltpu.roll(left, HALF, 1), right)
    packed = jnp.concatenate([lower, upper], axis=0)
    slot = lax.broadcasted_iota(jnp.int32, packed.shape, 1) % HALF // 4
    high = packed.astype(jnp.bfloat16).astype(jnp.float32)
    low = packed - high
    low = jnp.where(slot % 2 == 0, pltpu.roll(low, WIDTH - 4, 1), pltpu.roll(low, 4, 1))
    high, low = high.astype(jnp.bfloat16), low.astype(jnp.bfloat16)
    slot = slot.astype(jnp.bfloat16)
    zero = jnp.zeros_like(high)
    weights = weights_ref[...]
    sums = jnp.zeros((8, WIDTH), jnp.float32)
    for p in range(CHUNKS // 2):
        mine = jnp.where(slot == p, high, zero)
        rows = jnp.concatenate([jnp.where(slot == (p ^ 1), low, mine), mine], axis=1)
        out = jnp.dot(rows, weights, preferred_element_type=jnp.float32)
        for e in range(2):
            part = pl.ds((2 * p + e) * count, count)
            value = solved_ref[part, :] + out[:, e * WIDTH : (e + 1) * WIDTH]
            out_ref[part, :] = value
            sums = sums + jnp.sum((value * value).reshape(count // 8, 8, WIDTH), axis=0)
    sums_ref[...] = jnp.sum(sums, axis=0, keepdims=True)


def flush_kernel(start, rows, values_ref, *refs):
    out_ref, sem = refs[-2:]
    part = pl.ds(start, rows)
    copy = pltpu.make_async_copy(values_ref.at[part], out_ref.at[part], sem)
    copy.start()
    copy.wait()


def local(velocity, metric):
    parts, lines, width = velocity.shape
    rows = parts * lines
    count = rows // CHUNKS
    blocks, across = lax.axis_size("blk"), lax.axis_size("lines")
    assert width == WIDTH and rows % (CHUNKS * 32) == 0 and blocks % 2 == 0
    vmem = pl.BlockSpec(memory_space=pltpu.VMEM)
    hbm = pl.BlockSpec(memory_space=pltpu.HBM)
    in_hbm = functools.partial(pltpu.with_memory_space_constraint, memory_space=pltpu.HBM)
    params = pltpu.CompilerParams(vmem_limit_bytes=LIMIT)
    f32 = jnp.float32
    sizes = [8, 8, 8, 8]
    stations, outer, inner = pl.pallas_call(
        functools.partial(edges_kernel, sizes),
        out_shape=(
            pltpu.VMEM((rows, width), f32),
            pltpu.VMEM((count // 2, width), f32),
            pltpu.VMEM((count // 2, width), f32),
        ),
        in_specs=[hbm] * 3,
        out_specs=(vmem, vmem, vmem),
        scratch_shapes=[
            pltpu.VMEM((count, width), f32),
            pltpu.VMEM((count, width), f32),
            pltpu.VMEM((width, 2 * width), jnp.bfloat16),
            pltpu.VMEM((width, width), jnp.bfloat16),
            pltpu.SemaphoreType.DMA((len(sizes) + 2,)),
        ],
        compiler_params=params,
        name="edges",
    )(in_hbm(velocity.reshape(rows, width)), in_hbm(jnp.asarray(edge_weights())), in_hbm(jnp.asarray(low_weights())))
    far = [(i, (i + 1) % blocks) for i in range(1, blocks, 2)]
    outer = lax.ppermute(outer, "blk", far + [(j, i) for i, j in far])
    inner = lax.ppermute(inner, "blk", [(i, i ^ 1) for i in range(blocks)])
    solved, scaled = pl.pallas_call(
        local_kernel,
        out_shape=(pltpu.VMEM((rows, width), f32), pltpu.VMEM((2 * width, 2 * width), jnp.bfloat16)),
        in_specs=[vmem] * 4,
        out_specs=(vmem, vmem),
        compiler_params=params,
        name="local",
    )(stations, jnp.asarray(local_weights()), jnp.asarray(reach_rows()), metric.reshape(1, width))
    values, sums = pl.pallas_call(
        reach_kernel,
        out_shape=(pltpu.VMEM((rows, width), f32), pltpu.VMEM((1, width), f32)),
        in_specs=[vmem] * 4,
        out_specs=(vmem, vmem),
        compiler_params=params,
        name="reach",
    )(solved, outer, inner, scaled)

    def flush(start, size, *derivs):
        return pl.pallas_call(
            functools.partial(flush_kernel, start, size),
            out_shape=pltpu.HBM((rows, width), f32),
            in_specs=[vmem] + [hbm] * len(derivs),
            out_specs=hbm,
            scratch_shapes=[pltpu.SemaphoreType.DMA],
            input_output_aliases={1: 0} if derivs else {},
            compiler_params=params,
            name="flush",
        )(values, *derivs)

    derivs = flush(0, rows // 2)
    if across & (across - 1) == 0:
        step = 1
        while step < across:
            other = lax.ppermute(sums, "lines", [(i, i ^ step) for i in range(across)])
            if step == 1:
                other, derivs = lax.optimization_barrier((other, derivs))
            sums = sums + other
            step *= 2
    else:
        sums = lax.psum(sums, "lines")
    derivs = flush(rows // 2, rows - rows // 2, derivs)
    profile = sums.reshape(width) / (lines * across)
    return derivs.reshape(velocity.shape), profile


def solution(mesh):
    in_specs = (P(None, "lines", "blk"), P("blk"))
    out_specs = (P(None, "lines", "blk"), P("blk"))
    return jax.shard_map(local, mesh=mesh, in_specs=in_specs, out_specs=out_specs, check_vma=False)
```

```python
import functools

import jax
import jax.numpy as jnp
import ml_dtypes
import numpy as np
from jax import lax
from jax.experimental import pallas as pl
from jax.experimental.pallas import tpu as pltpu
from jax.sharding import PartitionSpec as P

ALPHA = 1.0 / 3.0
COEF_A = 7.0 / 9.0
COEF_B = 1.0 / 36.0

ROOT = np.sqrt(1.0 - 4.0 * ALPHA * ALPHA)
RATIO = (1.0 - ROOT) / (2.0 * ALPHA)
NEAR = COEF_B / ALPHA
GAIN = (COEF_A - NEAR) / ROOT * (1.0 / RATIO - RATIO)

WIDTH = 128
HALF = WIDTH // 2
CHUNKS = 32
EDGE = 16
LIMIT = 24 * 2**20


def powers(exponents):
    return (-RATIO) ** np.asarray(exponents, np.float64)


def split(matrix):
    high = matrix.astype(np.float32).astype(ml_dtypes.bfloat16)
    low = (matrix - high.astype(np.float64)).astype(np.float32).astype(ml_dtypes.bfloat16)
    return high, low


def local_weights():
    lag = np.arange(WIDTH)[None, :] - np.arange(WIDTH)[:, None]
    weights = np.sign(lag) * (GAIN * powers(np.abs(lag)) - NEAR * (np.abs(lag) == 1))
    return np.concatenate(split(weights), axis=1)


def edge_columns():
    station = np.arange(WIDTH)
    columns = [powers(station), station == 0, powers(WIDTH - 1 - station), station == WIDTH - 1]
    weights = np.zeros((WIDTH, WIDTH))
    for lane in range(WIDTH):
        weights[:, lane] = columns[2 * (lane // HALF) + lane % 2]
    return weights


def edge_weights():
    return np.concatenate(split(edge_columns()), axis=1)


def low_weights():
    weights = np.zeros((WIDTH, WIDTH))
    columns = edge_columns()
    for station in list(range(EDGE)) + list(range(WIDTH - EDGE, WIDTH)):
        for lane in range(WIDTH):
            chunk = lane % HALF // 2
            weights[(station + 2 * EDGE * (chunk % 4)) % WIDTH, lane] = columns[station, lane]
    return split(weights)[0]


def reach_rows():
    station = np.arange(WIDTH)
    rows = [GAIN * powers(station + 1), -NEAR * (station == 0), -GAIN * powers(WIDTH - station), NEAR * (station == WIDTH - 1)]
    return np.stack(rows).astype(np.float32)


def parity():
    return lax.rem(lax.axis_index("blk"), 2)


def halves(value):
    high = value.astype(jnp.bfloat16)
    return high, (value - high.astype(jnp.float32)).astype(jnp.bfloat16)


def edges_kernel(sizes, velocity_hbm, weights_hbm, lows_hbm, velocity_ref, outer_ref, inner_ref, packed, small, weights_ref, lows_ref, sems):
    count = velocity_ref.shape[0] // CHUNKS
    fetch = pltpu.make_async_copy(weights_hbm, weights_ref, sems.at[len(sizes)])
    fetch_lows = pltpu.make_async_copy(lows_hbm, lows_ref, sems.at[len(sizes) + 1])
    copies, firsts = [], np.cumsum([0] + sizes)
    for g, size in enumerate(sizes):
        part = pl.ds(int(firsts[g]) * count, size * count)
        copies.append(pltpu.make_async_copy(velocity_hbm.at[part], velocity_ref.at[part], sems.at[g]))
    copies[0].start()
    fetch.start()
    fetch_lows.start()
    for copy in copies[1:]:
        copy.start()
    fetch.wait()
    fetch_lows.wait()
    weights = weights_ref[...]
    odd = lax.broadcasted_iota(jnp.int32, weights.shape, 1) % 4 // 2
    zero = jnp.zeros_like(weights)
    odd = odd.astype(jnp.bfloat16)
    weights = jnp.concatenate([jnp.where(odd == 0, weights, zero), jnp.where(odd == 0, zero, weights)], axis=0)
    lows = lows_ref[...]
    lane = lax.broadcasted_iota(jnp.int32, (count, WIDTH), 1)
    owner = lane % HALF // 2
    for g, copy in enumerate(copies):
        copy.wait()
        for first in range(int(firsts[g]), int(firsts[g + 1]), 4):
            for pair in range(2):
                highs = []
                for e in range(2):
                    turn = 2 * pair + e
                    value = velocity_ref[pl.ds((first + turn) * count, count), :]
                    highs.append(value.astype(jnp.bfloat16))
                    low = value - highs[-1].astype(jnp.float32)
                    if turn == 0:
                        merged = low
                    else:
                        inside = (lane + WIDTH + EDGE - 2 * EDGE * turn) % WIDTH < 2 * EDGE
                        merged = jnp.where(inside, pltpu.roll(low, 2 * EDGE * turn, 1), merged)
                out = jnp.dot(jnp.concatenate(highs, axis=1), weights, preferred_element_type=jnp.float32)
                pltpu.store(packed, out[:, :WIDTH] + out[:, WIDTH:], mask=owner // 2 == first // 2 + pair)
            out = jnp.dot(merged.astype(jnp.bfloat16), lows, preferred_element_type=jnp.float32)
            pltpu.store(small, out, mask=owner // 4 == first // 4)
    lower = packed[: count // 2, :] + small[: count // 2, :]
    upper = packed[count // 2 :, :] + small[count // 2 :, :]
    lane = lane[: count // 2]
    first = jnp.where(lane < HALF, lower, pltpu.roll(upper, HALF, 1))
    last = jnp.where(lane < HALF, pltpu.roll(lower, HALF, 1), upper)
    even = parity() == 0
    outer_ref[...] = jnp.where(even, first, last)
    inner_ref[...] = jnp.where(even, last, first)


def reach_weights(rows, side):
    lane = lax.broadcasted_iota(jnp.int32, (WIDTH, WIDTH), 0)
    pick = [jnp.where(side == 0, rows[q : q + 1, :], rows[q + 2 : q + 3, :]) for q in range(2)]
    spread = jnp.where(lane % 2 == 0, pick[0], pick[1])
    high = spread.astype(jnp.bfloat16).astype(jnp.float32)
    spread = jnp.where(lane // 4 % 2 == 0, high, spread - high)
    zero = jnp.zeros_like(spread)
    first = lane % 4 // 2 == 0
    both = jnp.concatenate([jnp.where(first, spread, zero), jnp.where(first, zero, spread)], axis=1)
    return both.astype(jnp.bfloat16)


def reach(values, weights):
    slot = lax.broadcasted_iota(jnp.int32, values.shape, 1) // 4
    high = values.astype(jnp.bfloat16).astype(jnp.float32)
    low = values - high
    even = slot % 2 == 0
    highs = [jnp.where(even, high, pltpu.roll(high, 4, 1)), jnp.where(even, pltpu.roll(high, WIDTH - 4, 1), high)]
    lows = [pltpu.roll(low, 8, 1), pltpu.roll(low, 4, 1)]
    highs = [x.astype(jnp.bfloat16) for x in highs]
    lows = [x.astype(jnp.bfloat16) for x in lows]
    pair = (slot // 2).astype(jnp.bfloat16)
    slot = slot.astype(jnp.bfloat16)
    zero = jnp.zeros_like(lows[0])
    slots = WIDTH // 4
    for k in range(slots // 2):
        rows = []
        for s in (k, k + slots // 2):
            mine = jnp.where(slot == (2 * (s // 2) + 2) % slots, lows[k % 2], zero)
            rows.append(jnp.where(pair == s // 2, highs[k % 2], mine))
        yield k, jnp.dot(jnp.concatenate(rows, axis=0), weights, preferred_element_type=jnp.float32)


def near_kernel(velocity_ref, inner_ref, weights_ref, rows_ref, metric_ref, out_ref, far_ref):
    count = velocity_ref.shape[0] // CHUNKS
    weights = jnp.concatenate([weights_ref[...]] * 2, axis=0)
    metric = jnp.broadcast_to(metric_ref[...], (count, WIDTH))
    scaled = rows_ref[...] * metric_ref[...]
    far_ref[...] = reach_weights(scaled, parity())
    for k, added in reach(inner_ref[...], reach_weights(scaled, 1 - parity())):
        for e in range(2):
            part = pl.ds((2 * k + e) * count, count)
            both = jnp.concatenate(halves(velocity_ref[part, :]), axis=1)
            out = jnp.dot(both, weights, preferred_element_type=jnp.float32)
            out_ref[part, :] = (out[:, :WIDTH] + out[:, WIDTH:]) * metric + added[:, e * WIDTH : (e + 1) * WIDTH]


def far_kernel(solved_ref, outer_ref, weights_ref, out_ref, sums_ref):
    count = solved_ref.shape[0] // CHUNKS
    sums = jnp.zeros((8, WIDTH), jnp.float32)
    for k, added in reach(outer_ref[...], weights_ref[...]):
        for e in range(2):
            part = pl.ds((2 * k + e) * count, count)
            value = solved_ref[part, :] + added[:, e * WIDTH : (e + 1) * WIDTH]
            out_ref[part, :] = value
            sums = sums + jnp.sum((value * value).reshape(count // 8, 8, WIDTH), axis=0)
    sums_ref[...] = jnp.sum(sums, axis=0, keepdims=True)


def flush_kernel(start, rows, values_ref, *refs):
    out_ref, sem = refs[-2:]
    part = pl.ds(start, rows)
    copy = pltpu.make_async_copy(values_ref.at[part], out_ref.at[part], sem)
    copy.start()
    copy.wait()


def local(velocity, metric):
    parts, lines, width = velocity.shape
    rows = parts * lines
    count = rows // CHUNKS
    blocks, across = lax.axis_size("blk"), lax.axis_size("lines")
    assert width == WIDTH and rows % (CHUNKS * 32) == 0 and blocks % 2 == 0
    vmem = pl.BlockSpec(memory_space=pltpu.VMEM)
    hbm = pl.BlockSpec(memory_space=pltpu.HBM)
    in_hbm = functools.partial(pltpu.with_memory_space_constraint, memory_space=pltpu.HBM)
    params = pltpu.CompilerParams(vmem_limit_bytes=LIMIT)
    f32 = jnp.float32
    sizes = [8, 8, 8, 8]
    stations, outer, inner = pl.pallas_call(
        functools.partial(edges_kernel, sizes),
        out_shape=(
            pltpu.VMEM((rows, width), f32),
            pltpu.VMEM((count // 2, width), f32),
            pltpu.VMEM((count // 2, width), f32),
        ),
        in_specs=[hbm] * 3,
        out_specs=(vmem, vmem, vmem),
        scratch_shapes=[
            pltpu.VMEM((count, width), f32),
            pltpu.VMEM((count, width), f32),
            pltpu.VMEM((width, 2 * width), jnp.bfloat16),
            pltpu.VMEM((width, width), jnp.bfloat16),
            pltpu.SemaphoreType.DMA((len(sizes) + 2,)),
        ],
        compiler_params=params,
        name="edges",
    )(in_hbm(velocity.reshape(rows, width)), in_hbm(jnp.asarray(edge_weights())), in_hbm(jnp.asarray(low_weights())))
    far = [(i, (i + 1) % blocks) for i in range(1, blocks, 2)]
    outer = lax.ppermute(outer, "blk", far + [(j, i) for i, j in far])
    inner = lax.ppermute(inner, "blk", [(i, i ^ 1) for i in range(blocks)])
    solved, weights = pl.pallas_call(
        near_kernel,
        out_shape=(pltpu.VMEM((rows, width), f32), pltpu.VMEM((width, 2 * width), jnp.bfloat16)),
        in_specs=[vmem] * 5,
        out_specs=(vmem, vmem),
        compiler_params=params,
        name="near",
    )(stations, inner, jnp.asarray(local_weights()), jnp.asarray(reach_rows()), metric.reshape(1, width))
    values, sums = pl.pallas_call(
        far_kernel,
        out_shape=(pltpu.VMEM((rows, width), f32), pltpu.VMEM((1, width), f32)),
        in_specs=[vmem] * 3,
        out_specs=(vmem, vmem),
        compiler_params=params,
        name="far",
    )(solved, outer, weights)

    def flush(start, size, *derivs):
        return pl.pallas_call(
            functools.partial(flush_kernel, start, size),
            out_shape=pltpu.HBM((rows, width), f32),
            in_specs=[vmem] + [hbm] * len(derivs),
            out_specs=hbm,
            scratch_shapes=[pltpu.SemaphoreType.DMA],
            input_output_aliases={1: 0} if derivs else {},
            compiler_params=params,
            name="flush",
        )(values, *derivs)

    derivs = flush(0, rows // 2)
    if across & (across - 1) == 0:
        step = 1
        while step < across:
            other = lax.ppermute(sums, "lines", [(i, i ^ step) for i in range(across)])
            if step == 1:
                other, derivs = lax.optimization_barrier((other, derivs))
            sums = sums + other
            step *= 2
    else:
        sums = lax.psum(sums, "lines")
    derivs = flush(rows // 2, rows - rows // 2, derivs)
    profile = sums.reshape(width) / (lines * across)
    return derivs.reshape(velocity.shape), profile


def solution(mesh):
    in_specs = (P(None, "lines", "blk"), P("blk"))
    out_specs = (P(None, "lines", "blk"), P("blk"))
    return jax.shard_map(local, mesh=mesh, in_specs=in_specs, out_specs=out_specs, check_vma=False)
```

```python
import functools

import jax
import jax.numpy as jnp
import ml_dtypes
import numpy as np
from jax import lax
from jax.experimental import pallas as pl
from jax.experimental.pallas import tpu as pltpu
from jax.sharding import PartitionSpec as P

ALPHA = 1.0 / 3.0
COEF_A = 7.0 / 9.0
COEF_B = 1.0 / 36.0

ROOT = np.sqrt(1.0 - 4.0 * ALPHA * ALPHA)
RATIO = (1.0 - ROOT) / (2.0 * ALPHA)
NEAR = COEF_B / ALPHA
GAIN = (COEF_A - NEAR) / ROOT * (1.0 / RATIO - RATIO)

WIDTH = 128
HALF = WIDTH // 2
CHUNKS = 32
EDGE = 16
LIMIT = 24 * 2**20


def powers(exponents):
    return (-RATIO) ** np.asarray(exponents, np.float64)


def split(matrix):
    high = matrix.astype(np.float32).astype(ml_dtypes.bfloat16)
    low = (matrix - high.astype(np.float64)).astype(np.float32).astype(ml_dtypes.bfloat16)
    return high, low


def local_weights():
    lag = np.arange(WIDTH)[None, :] - np.arange(WIDTH)[:, None]
    weights = np.sign(lag) * (GAIN * powers(np.abs(lag)) - NEAR * (np.abs(lag) == 1))
    return np.concatenate(split(weights), axis=1)


def edge_columns():
    station = np.arange(WIDTH)
    columns = [powers(station), station == 0, powers(WIDTH - 1 - station), station == WIDTH - 1]
    weights = np.zeros((WIDTH, WIDTH))
    for lane in range(WIDTH):
        weights[:, lane] = columns[2 * (lane // HALF) + lane % 2]
    return weights


def edge_weights():
    return np.concatenate(split(edge_columns()), axis=1)


def low_weights():
    weights = np.zeros((WIDTH, WIDTH))
    columns = edge_columns()
    for station in list(range(EDGE)) + list(range(WIDTH - EDGE, WIDTH)):
        for lane in range(WIDTH):
            chunk = lane % HALF // 2
            weights[(station + 2 * EDGE * (chunk % 4)) % WIDTH, lane] = columns[station, lane]
    return split(weights)[0]


def reach_rows():
    station = np.arange(WIDTH)
    rows = [GAIN * powers(station + 1), -NEAR * (station == 0), -GAIN * powers(WIDTH - station), NEAR * (station == WIDTH - 1)]
    return np.stack(rows).astype(np.float32)


def parity():
    return lax.rem(lax.axis_index("blk"), 2)


def halves(value):
    high = value.astype(jnp.bfloat16)
    return high, (value - high.astype(jnp.float32)).astype(jnp.bfloat16)


def edges_kernel(sizes, velocity_hbm, weights_hbm, lows_hbm, velocity_ref, outer_ref, inner_ref, packed, small, weights_ref, lows_ref, sems):
    count = velocity_ref.shape[0] // CHUNKS
    fetch = pltpu.make_async_copy(weights_hbm, weights_ref, sems.at[len(sizes)])
    fetch_lows = pltpu.make_async_copy(lows_hbm, lows_ref, sems.at[len(sizes) + 1])
    copies, firsts = [], np.cumsum([0] + sizes)
    for g, size in enumerate(sizes):
        part = pl.ds(int(firsts[g]) * count, size * count)
        copies.append(pltpu.make_async_copy(velocity_hbm.at[part], velocity_ref.at[part], sems.at[g]))
    copies[0].start()
    fetch.start()
    fetch_lows.start()
    for copy in copies[1:]:
        copy.start()
    fetch.wait()
    fetch_lows.wait()
    weights = weights_ref[...]
    odd = lax.broadcasted_iota(jnp.int32, weights.shape, 1) % 4 // 2
    zero = jnp.zeros_like(weights)
    odd = odd.astype(jnp.bfloat16)
    weights = jnp.concatenate([jnp.where(odd == 0, weights, zero), jnp.where(odd == 0, zero, weights)], axis=0)
    lows = lows_ref[...]
    lane = lax.broadcasted_iota(jnp.int32, (count, WIDTH), 1)
    owner = lane % HALF // 2
    size = sizes[0]

    def group(g, carry):
        start = pl.multiple_of(g * (size * count), size * count)
        part = pl.ds(start, size * count)
        pltpu.make_async_copy(velocity_hbm.at[part], velocity_ref.at[part], sems.at[g]).wait()
        for first in range(0, size, 4):
            for pair in range(2):
                highs = []
                for e in range(2):
                    turn = 2 * pair + e
                    value = velocity_ref[pl.ds(start + (first + turn) * count, count), :]
                    highs.append(value.astype(jnp.bfloat16))
                    low = value - highs[-1].astype(jnp.float32)
                    if turn == 0:
                        merged = low
                    else:
                        inside = (lane + WIDTH + EDGE - 2 * EDGE * turn) % WIDTH < 2 * EDGE
                        merged = jnp.where(inside, pltpu.roll(low, 2 * EDGE * turn, 1), merged)
                out = jnp.dot(jnp.concatenate(highs, axis=1), weights, preferred_element_type=jnp.float32)
                pltpu.store(packed, out[:, :WIDTH] + out[:, WIDTH:], mask=owner // 2 == g * (size // 2) + first // 2 + pair)
            out = jnp.dot(merged.astype(jnp.bfloat16), lows, preferred_element_type=jnp.float32)
            pltpu.store(small, out, mask=owner // 4 == g * (size // 4) + first // 4)
        return carry

    lax.fori_loop(0, len(sizes), group, 0)
    lower = packed[: count // 2, :] + small[: count // 2, :]
    upper = packed[count // 2 :, :] + small[count // 2 :, :]
    lane = lane[: count // 2]
    first = jnp.where(lane < HALF, lower, pltpu.roll(upper, HALF, 1))
    last = jnp.where(lane < HALF, pltpu.roll(lower, HALF, 1), upper)
    even = parity() == 0
    outer_ref[...] = jnp.where(even, first, last)
    inner_ref[...] = jnp.where(even, last, first)


def reach_weights(rows, side):
    lane = lax.broadcasted_iota(jnp.int32, (WIDTH, WIDTH), 0)
    pick = [jnp.where(side == 0, rows[q : q + 1, :], rows[q + 2 : q + 3, :]) for q in range(2)]
    spread = jnp.where(lane % 2 == 0, pick[0], pick[1])
    high = spread.astype(jnp.bfloat16).astype(jnp.float32)
    spread = jnp.where(lane // 4 % 2 == 0, high, spread - high)
    zero = jnp.zeros_like(spread)
    first = lane % 4 // 2 == 0
    both = jnp.concatenate([jnp.where(first, spread, zero), jnp.where(first, zero, spread)], axis=1)
    return both.astype(jnp.bfloat16)


def reach(values, weights):
    slot = lax.broadcasted_iota(jnp.int32, values.shape, 1) // 4
    high, low = halves(values)
    even = (slot % 2).astype(jnp.bfloat16) == 0
    highs = [jnp.where(even, high, pltpu.roll(high, 4, 1)), jnp.where(even, pltpu.roll(high, WIDTH - 4, 1), high)]
    lows = [pltpu.roll(low, 8, 1), pltpu.roll(low, 4, 1)]
    pair = (slot // 2).astype(jnp.bfloat16)
    slot = slot.astype(jnp.bfloat16)
    zero = jnp.zeros_like(lows[0])
    slots = WIDTH // 4
    for k in range(slots // 2):
        rows = []
        for s in (k, k + slots // 2):
            mine = jnp.where(slot == (2 * (s // 2) + 2) % slots, lows[k % 2], zero)
            rows.append(jnp.where(pair == s // 2, highs[k % 2], mine))
        yield k, jnp.dot(jnp.concatenate(rows, axis=0), weights, preferred_element_type=jnp.float32)


def near_kernel(velocity_ref, inner_ref, weights_ref, rows_ref, metric_ref, out_ref, far_ref):
    count = velocity_ref.shape[0] // CHUNKS
    weights = jnp.concatenate([weights_ref[...]] * 2, axis=0)
    metric = jnp.broadcast_to(metric_ref[...], (count, WIDTH))
    scaled = rows_ref[...] * metric_ref[...]
    far_ref[...] = reach_weights(scaled, parity())
    for k, added in reach(inner_ref[...], reach_weights(scaled, 1 - parity())):
        for e in range(2):
            part = pl.ds((2 * k + e) * count, count)
            both = jnp.concatenate(halves(velocity_ref[part, :]), axis=1)
            out = jnp.dot(both, weights, preferred_element_type=jnp.float32)
            out_ref[part, :] = (out[:, :WIDTH] + out[:, WIDTH:]) * metric + added[:, e * WIDTH : (e + 1) * WIDTH]


def far_kernel(solved_ref, outer_ref, weights_ref, out_ref, sums_ref):
    count = solved_ref.shape[0] // CHUNKS
    sums = jnp.zeros((8, WIDTH), jnp.float32)
    for k, added in reach(outer_ref[...], weights_ref[...]):
        for e in range(2):
            part = pl.ds((2 * k + e) * count, count)
            value = solved_ref[part, :] + added[:, e * WIDTH : (e + 1) * WIDTH]
            out_ref[part, :] = value
            sums = sums + jnp.sum((value * value).reshape(count // 8, 8, WIDTH), axis=0)
    sums_ref[...] = jnp.sum(sums, axis=0, keepdims=True)


def flush_kernel(start, rows, values_ref, *refs):
    out_ref, sem = refs[-2:]
    part = pl.ds(start, rows)
    copy = pltpu.make_async_copy(values_ref.at[part], out_ref.at[part], sem)
    copy.start()
    copy.wait()


def local(velocity, metric):
    parts, lines, width = velocity.shape
    rows = parts * lines
    count = rows // CHUNKS
    blocks, across = lax.axis_size("blk"), lax.axis_size("lines")
    assert width == WIDTH and rows % (CHUNKS * 32) == 0 and blocks % 2 == 0
    vmem = pl.BlockSpec(memory_space=pltpu.VMEM)
    hbm = pl.BlockSpec(memory_space=pltpu.HBM)
    in_hbm = functools.partial(pltpu.with_memory_space_constraint, memory_space=pltpu.HBM)
    params = pltpu.CompilerParams(vmem_limit_bytes=LIMIT)
    f32 = jnp.float32
    sizes = [8, 8, 8, 8]
    stations, outer, inner = pl.pallas_call(
        functools.partial(edges_kernel, sizes),
        out_shape=(
            pltpu.VMEM((rows, width), f32),
            pltpu.VMEM((count // 2, width), f32),
            pltpu.VMEM((count // 2, width), f32),
        ),
        in_specs=[hbm] * 3,
        out_specs=(vmem, vmem, vmem),
        scratch_shapes=[
            pltpu.VMEM((count, width), f32),
            pltpu.VMEM((count, width), f32),
            pltpu.VMEM((width, 2 * width), jnp.bfloat16),
            pltpu.VMEM((width, width), jnp.bfloat16),
            pltpu.SemaphoreType.DMA((len(sizes) + 2,)),
        ],
        compiler_params=params,
        name="edges",
    )(in_hbm(velocity.reshape(rows, width)), in_hbm(jnp.asarray(edge_weights())), in_hbm(jnp.asarray(low_weights())))
    far = [(i, (i + 1) % blocks) for i in range(1, blocks, 2)]
    outer = lax.ppermute(outer, "blk", far + [(j, i) for i, j in far])
    inner = lax.ppermute(inner, "blk", [(i, i ^ 1) for i in range(blocks)])
    solved, weights = pl.pallas_call(
        near_kernel,
        out_shape=(pltpu.VMEM((rows, width), f32), pltpu.VMEM((width, 2 * width), jnp.bfloat16)),
        in_specs=[vmem] * 5,
        out_specs=(vmem, vmem),
        compiler_params=params,
        name="near",
    )(stations, inner, jnp.asarray(local_weights()), jnp.asarray(reach_rows()), metric.reshape(1, width))
    values, sums = pl.pallas_call(
        far_kernel,
        out_shape=(pltpu.VMEM((rows, width), f32), pltpu.VMEM((1, width), f32)),
        in_specs=[vmem] * 3,
        out_specs=(vmem, vmem),
        compiler_params=params,
        name="far",
    )(solved, outer, weights)

    def flush(start, size, *derivs):
        return pl.pallas_call(
            functools.partial(flush_kernel, start, size),
            out_shape=pltpu.HBM((rows, width), f32),
            in_specs=[vmem] + [hbm] * len(derivs),
            out_specs=hbm,
            scratch_shapes=[pltpu.SemaphoreType.DMA],
            input_output_aliases={1: 0} if derivs else {},
            compiler_params=params,
            name="flush",
        )(values, *derivs)

    derivs = flush(0, rows // 2)
    if across & (across - 1) == 0:
        step = 1
        while step < across:
            other = lax.ppermute(sums, "lines", [(i, i ^ step) for i in range(across)])
            if step == 1:
                other, derivs = lax.optimization_barrier((other, derivs))
            sums = sums + other
            step *= 2
    else:
        sums = lax.psum(sums, "lines")
    derivs = flush(rows // 2, rows - rows // 2, derivs)
    profile = sums.reshape(width) / (lines * across)
    return derivs.reshape(velocity.shape), profile


def solution(mesh):
    in_specs = (P(None, "lines", "blk"), P("blk"))
    out_specs = (P(None, "lines", "blk"), P("blk"))
    return jax.shard_map(local, mesh=mesh, in_specs=in_specs, out_specs=out_specs, check_vma=False)
```

```python
import functools

import jax
import jax.numpy as jnp
import ml_dtypes
import numpy as np
from jax import lax
from jax.experimental import pallas as pl
from jax.experimental.pallas import tpu as pltpu
from jax.sharding import PartitionSpec as P

ALPHA = 1.0 / 3.0
COEF_A = 7.0 / 9.0
COEF_B = 1.0 / 36.0

ROOT = np.sqrt(1.0 - 4.0 * ALPHA * ALPHA)
RATIO = (1.0 - ROOT) / (2.0 * ALPHA)
NEAR = COEF_B / ALPHA
GAIN = (COEF_A - NEAR) / ROOT * (1.0 / RATIO - RATIO)

WIDTH = 128
HALF = WIDTH // 2
CHUNKS = 32
EDGE = 16
LIMIT = 24 * 2**20


def powers(exponents):
    return (-RATIO) ** np.asarray(exponents, np.float64)


def split(matrix):
    high = matrix.astype(np.float32).astype(ml_dtypes.bfloat16)
    low = (matrix - high.astype(np.float64)).astype(np.float32).astype(ml_dtypes.bfloat16)
    return high, low


def local_weights():
    lag = np.arange(WIDTH)[None, :] - np.arange(WIDTH)[:, None]
    weights = np.sign(lag) * (GAIN * powers(np.abs(lag)) - NEAR * (np.abs(lag) == 1))
    return np.concatenate(split(weights), axis=1)


def edge_columns():
    station = np.arange(WIDTH)
    columns = [powers(station), station == 0, powers(WIDTH - 1 - station), station == WIDTH - 1]
    weights = np.zeros((WIDTH, WIDTH))
    for lane in range(WIDTH):
        weights[:, lane] = columns[2 * (lane // HALF) + lane % 2]
    return weights


def edge_weights():
    return np.concatenate(split(edge_columns()), axis=1)


def low_weights():
    weights = np.zeros((WIDTH, WIDTH))
    columns = edge_columns()
    for station in list(range(EDGE)) + list(range(WIDTH - EDGE, WIDTH)):
        for lane in range(WIDTH):
            chunk = lane % HALF // 2
            weights[(station + 2 * EDGE * (chunk % 4)) % WIDTH, lane] = columns[station, lane]
    return split(weights)[0]


def reach_rows():
    station = np.arange(WIDTH)
    rows = [GAIN * powers(station + 1), -NEAR * (station == 0), -GAIN * powers(WIDTH - station), NEAR * (station == WIDTH - 1)]
    return np.stack(rows).astype(np.float32)


def parity():
    return lax.rem(lax.axis_index("blk"), 2)


def halves(value):
    high = value.astype(jnp.bfloat16)
    return high, (value - high.astype(jnp.float32)).astype(jnp.bfloat16)


def edges_kernel(sizes, velocity_hbm, weights_hbm, lows_hbm, velocity_ref, outer_ref, inner_ref, packed, small, weights_ref, lows_ref, sems):
    count = velocity_ref.shape[0] // CHUNKS
    fetch = pltpu.make_async_copy(weights_hbm, weights_ref, sems.at[len(sizes)])
    fetch_lows = pltpu.make_async_copy(lows_hbm, lows_ref, sems.at[len(sizes) + 1])
    copies, firsts = [], np.cumsum([0] + sizes)
    for g, size in enumerate(sizes):
        part = pl.ds(int(firsts[g]) * count, size * count)
        copies.append(pltpu.make_async_copy(velocity_hbm.at[part], velocity_ref.at[part], sems.at[g]))
    copies[0].start()
    fetch.start()
    fetch_lows.start()
    for copy in copies[1:]:
        copy.start()
    fetch.wait()
    fetch_lows.wait()
    weights = weights_ref[...]
    odd = lax.broadcasted_iota(jnp.int32, weights.shape, 1) % 4 // 2
    zero = jnp.zeros_like(weights)
    odd = odd.astype(jnp.bfloat16)
    weights = jnp.concatenate([jnp.where(odd == 0, weights, zero), jnp.where(odd == 0, zero, weights)], axis=0)
    lows = lows_ref[...]
    lane = lax.broadcasted_iota(jnp.int32, (count, WIDTH), 1)
    owner = lane % HALF // 2
    size = sizes[0]

    def group(g, carry):
        start = pl.multiple_of(g * (size * count), size * count)
        part = pl.ds(start, size * count)
        pltpu.make_async_copy(velocity_hbm.at[part], velocity_ref.at[part], sems.at[g]).wait()
        for first in range(0, size, 4):
            for pair in range(2):
                highs = []
                for e in range(2):
                    turn = 2 * pair + e
                    value = velocity_ref[pl.ds(start + (first + turn) * count, count), :]
                    highs.append(value.astype(jnp.bfloat16))
                    low = value - highs[-1].astype(jnp.float32)
                    if turn == 0:
                        merged = low
                    else:
                        inside = (lane + WIDTH + EDGE - 2 * EDGE * turn) % WIDTH < 2 * EDGE
                        merged = jnp.where(inside, pltpu.roll(low, 2 * EDGE * turn, 1), merged)
                out = jnp.dot(jnp.concatenate(highs, axis=1), weights, preferred_element_type=jnp.float32)
                pltpu.store(packed, out[:, :WIDTH] + out[:, WIDTH:], mask=owner // 2 == g * (size // 2) + first // 2 + pair)
            out = jnp.dot(merged.astype(jnp.bfloat16), lows, preferred_element_type=jnp.float32)
            pltpu.store(small, out, mask=owner // 4 == g * (size // 4) + first // 4)
        return carry

    lax.fori_loop(0, len(sizes), group, 0)
    lower = packed[: count // 2, :] + small[: count // 2, :]
    upper = packed[count // 2 :, :] + small[count // 2 :, :]
    lane = lane[: count // 2]
    first = jnp.where(lane < HALF, lower, pltpu.roll(upper, HALF, 1))
    last = jnp.where(lane < HALF, pltpu.roll(lower, HALF, 1), upper)
    even = parity() == 0
    outer_ref[...] = jnp.where(even, first, last)
    inner_ref[...] = jnp.where(even, last, first)


def reach_weights(rows, side):
    lane = lax.broadcasted_iota(jnp.int32, (WIDTH, WIDTH), 0)
    pick = [jnp.where(side == 0, rows[q : q + 1, :], rows[q + 2 : q + 3, :]) for q in range(2)]
    spread = jnp.where(lane % 2 == 0, pick[0], pick[1])
    high = spread.astype(jnp.bfloat16).astype(jnp.float32)
    spread = jnp.where(lane // 4 % 2 == 0, high, spread - high)
    zero = jnp.zeros_like(spread)
    first = lane % 4 // 2 == 0
    both = jnp.concatenate([jnp.where(first, spread, zero), jnp.where(first, zero, spread)], axis=1)
    return both.astype(jnp.bfloat16)


def reach(values, weights):
    slot = lax.broadcasted_iota(jnp.int32, values.shape, 1) // 4
    high, low = halves(values)
    even = (slot % 2).astype(jnp.bfloat16) == 0
    highs = [jnp.where(even, high, pltpu.roll(high, 4, 1)), jnp.where(even, pltpu.roll(high, WIDTH - 4, 1), high)]
    lows = [pltpu.roll(low, 8, 1), pltpu.roll(low, 4, 1)]
    pair = (slot // 2).astype(jnp.bfloat16)
    slot = slot.astype(jnp.bfloat16)
    zero = jnp.zeros_like(lows[0])
    slots = WIDTH // 4
    for k in range(slots // 2):
        rows = []
        for s in (k, k + slots // 2):
            mine = jnp.where(slot == (2 * (s // 2) + 2) % slots, lows[k % 2], zero)
            rows.append(jnp.where(pair == s // 2, highs[k % 2], mine))
        yield k, jnp.dot(jnp.concatenate(rows, axis=0), weights, preferred_element_type=jnp.float32)


def near_kernel(velocity_ref, inner_ref, weights_ref, rows_ref, metric_ref, out_ref, far_ref):
    count = velocity_ref.shape[0] // CHUNKS
    weights = jnp.concatenate([weights_ref[...]] * 2, axis=0)
    metric = jnp.broadcast_to(metric_ref[...], (count, WIDTH))
    scaled = rows_ref[...] * metric_ref[...]
    far_ref[...] = reach_weights(scaled, parity())
    for k, added in reach(inner_ref[...], reach_weights(scaled, 1 - parity())):
        for e in range(2):
            part = pl.ds((2 * k + e) * count, count)
            both = jnp.concatenate(halves(velocity_ref[part, :]), axis=1)
            out = jnp.dot(both, weights, preferred_element_type=jnp.float32)
            out_ref[part, :] = (out[:, :WIDTH] + out[:, WIDTH:]) * metric + added[:, e * WIDTH : (e + 1) * WIDTH]


def far_kernel(solved_ref, outer_ref, weights_ref, out_ref, sums_ref):
    count = solved_ref.shape[0] // CHUNKS
    sums = jnp.zeros((8, WIDTH), jnp.float32)
    for k, added in reach(outer_ref[...], weights_ref[...]):
        for e in range(2):
            part = pl.ds((2 * k + e) * count, count)
            value = solved_ref[part, :] + added[:, e * WIDTH : (e + 1) * WIDTH]
            out_ref[part, :] = value
            sums = sums + jnp.sum((value * value).reshape(count // 8, 8, WIDTH), axis=0)
    sums_ref[...] = jnp.sum(sums, axis=0, keepdims=True)


def flush_kernel(start, rows, values_ref, *refs):
    out_ref, sem = refs[-2:]
    part = pl.ds(start, rows)
    copy = pltpu.make_async_copy(values_ref.at[part], out_ref.at[part], sem)
    copy.start()
    copy.wait()


def local(velocity, metric):
    parts, lines, width = velocity.shape
    rows = parts * lines
    count = rows // CHUNKS
    blocks, across = lax.axis_size("blk"), lax.axis_size("lines")
    assert width == WIDTH and rows % (CHUNKS * 32) == 0 and blocks % 2 == 0
    vmem = pl.BlockSpec(memory_space=pltpu.VMEM)
    hbm = pl.BlockSpec(memory_space=pltpu.HBM)
    in_hbm = functools.partial(pltpu.with_memory_space_constraint, memory_space=pltpu.HBM)
    params = pltpu.CompilerParams(vmem_limit_bytes=LIMIT)
    f32 = jnp.float32
    sizes = [8, 8, 8, 8]
    stations, outer, inner = pl.pallas_call(
        functools.partial(edges_kernel, sizes),
        out_shape=(
            pltpu.VMEM((rows, width), f32),
            pltpu.VMEM((count // 2, width), f32),
            pltpu.VMEM((count // 2, width), f32),
        ),
        in_specs=[hbm] * 3,
        out_specs=(vmem, vmem, vmem),
        scratch_shapes=[
            pltpu.VMEM((count, width), f32),
            pltpu.VMEM((count, width), f32),
            pltpu.VMEM((width, 2 * width), jnp.bfloat16),
            pltpu.VMEM((width, width), jnp.bfloat16),
            pltpu.SemaphoreType.DMA((len(sizes) + 2,)),
        ],
        compiler_params=params,
        name="edges",
    )(in_hbm(velocity.reshape(rows, width)), in_hbm(jnp.asarray(edge_weights())), in_hbm(jnp.asarray(low_weights())))
    far = [(i, (i + 1) % blocks) for i in range(1, blocks, 2)]
    outer = lax.ppermute(outer, "blk", far + [(j, i) for i, j in far])
    inner = lax.ppermute(inner, "blk", [(i, i ^ 1) for i in range(blocks)])
    solved, weights = pl.pallas_call(
        near_kernel,
        out_shape=(pltpu.VMEM((rows, width), f32), pltpu.VMEM((width, 2 * width), jnp.bfloat16)),
        in_specs=[vmem] * 5,
        out_specs=(vmem, vmem),
        compiler_params=params,
        name="near",
    )(stations, inner, jnp.asarray(local_weights()), jnp.asarray(reach_rows()), metric.reshape(1, width))
    values, sums = pl.pallas_call(
        far_kernel,
        out_shape=(pltpu.VMEM((rows, width), f32), pltpu.VMEM((1, width), f32)),
        in_specs=[vmem] * 3,
        out_specs=(vmem, vmem),
        compiler_params=params,
        name="far",
    )(solved, outer, weights)

    def flush(start, size, *derivs):
        return pl.pallas_call(
            functools.partial(flush_kernel, start, size),
            out_shape=pltpu.HBM((rows, width), f32),
            in_specs=[vmem] + [hbm] * len(derivs),
            out_specs=hbm,
            scratch_shapes=[pltpu.SemaphoreType.DMA],
            input_output_aliases={1: 0} if derivs else {},
            compiler_params=params,
            name="flush",
        )(values, *derivs)

    derivs = flush(0, rows // 2)
    if across & (across - 1) == 0:
        step = across // 2
        while step:
            other = lax.ppermute(sums, "lines", [(i, i ^ step) for i in range(across)])
            if step == across // 2:
                other, derivs = lax.optimization_barrier((other, derivs))
            sums = sums + other
            step //= 2
    else:
        sums = lax.psum(sums, "lines")
    derivs = flush(rows // 2, rows - rows // 2, derivs)
    profile = sums.reshape(width) / (lines * across)
    return derivs.reshape(velocity.shape), profile


def solution(mesh):
    in_specs = (P(None, "lines", "blk"), P("blk"))
    out_specs = (P(None, "lines", "blk"), P("blk"))
    return jax.shard_map(local, mesh=mesh, in_specs=in_specs, out_specs=out_specs, check_vma=False)
```
